32 devices in a mesh: group: 2 (over x), module: 16 (over z, y, core).
Axes of the slice: x: 2, y: 2, z: 4, core: 2. Of those that a mesh axis runs over, the one named last changes fastest.
Arguments:
- query_grads: float32 [16, 32, 128, 128], P(None, None, 'module'), may hold values from -0.1875 to 0.1875
- train_grads: float32 [32, 128, 128, 128], P('module', 'group'), parts along dimension 1, may hold values from -0.1875 to 0.1875
- out_basis: float32 [32, 128, 128], P('module'), may hold values from -0.5 to 0.5
- in_basis: float32 [32, 128, 128], P('module'), may hold values from -0.5 to 0.5
- corrections: float32 [32, 128, 128], P('module'), may hold values from 0.01 to 10
- ranks: int32 [16], replicated, may hold values from 32 to 128
- slot_modules: int32 [32], replicated, may hold values from -1 to 15, as said below
Outputs:
- scores: float32 [32, 128], P(None, 'group'), parts along dimension 1
The draws below stay inside these ranges and needn't reach their ends.
There are 2 independent parts, one for each index of `group`. The reference program is written for one: setup_inputs(seed, part) draws one part's arguments, and reference() takes and returns one part's arrays. A program takes and returns all parts, laid end to end along the dimension named above; an argument that names none is the same for every part. Nothing has to cross between parts.
Inputs may be any that keep to these rules, and one draw needn't show every extreme that they name: `slot_modules`: each module number 0 to 15 stands in exactly one entry; all other entries are -1. Owner i holds the 2 entries from i * 2 on, so an owner holds 0 to 2 modules, and some owner holds 2.
All inputs are finite; a program needn't handle non-finite values.
Results may differ from the reference program's by a relative error of at most 0.0003.
Values sent between devices are 32-bit elements; how exact they have to be, the bound alone decides.
No kernel may reach another device: no remote copies, remote signals or barrier semaphores. Data moves between devices by JAX's collectives and lax.ppermute only.
A program may use at most 128 MiB of HBM per device.

```python
import math
import jax
import jax.numpy as jnp
from jax import lax

DIM = 128
QUERIES = 32
EXAMPLES = 64
OWNER_SLOT_COUNT = 2
MODULES = 16
TOTAL_SLOT_ROWS = 32


def draw_slot_modules(key, part):
    order_key = jax.random.fold_in(key, 11)
    owner_key = jax.random.fold_in(key, 23)
    label_key = jax.random.fold_in(key, 37)
    ranking_keys = jax.random.permutation(order_key, TOTAL_SLOT_ROWS).astype(jnp.int32)
    selected_modules = jax.random.randint(owner_key, (), 0, TOTAL_SLOT_ROWS // OWNER_SLOT_COUNT)
    preference_boost = jnp.where(jnp.arange(TOTAL_SLOT_ROWS) // OWNER_SLOT_COUNT == selected_modules, TOTAL_SLOT_ROWS, 0).astype(jnp.int32)
    sorted_order = jnp.argsort(-(ranking_keys + preference_boost), stable=True)
    placement = jnp.argsort(sorted_order, stable=True).astype(jnp.int32)
    labels = jax.random.permutation(label_key, MODULES).astype(jnp.int32)
    picked = labels[jnp.clip(placement, 0, MODULES - 1)]
    return jnp.where(placement < MODULES, picked, -1).astype(jnp.int32)


def set_ends(drawn, stream_key, smallest, high):
    shape = drawn.shape
    index_at = [jax.random.randint(jax.random.fold_in(stream_key, axis), (), 0, shape[axis]) for axis in range(len(shape))]
    drawn = drawn.at[tuple(index_at)].set(smallest)
    longest = shape.index(max(shape))
    index_at[longest] = (index_at[longest] + 1) % shape[longest]
    return drawn.at[tuple(index_at)].set(high)


def levels(stream_key, extent, pieces, least, top_value):
    factor_of = 1.0
    for axis_at, shards_of in pieces:
        steps = jax.random.uniform(jax.random.fold_in(jax.random.fold_in(stream_key, 6), axis_at), (shards_of,), jnp.float32, least / len(pieces), top_value / len(pieces))
        factor_of = factor_of * jnp.repeat(jnp.exp(steps), extent[axis_at] // shards_of).reshape((-1,) + (1,) * (len(extent) - 1 - axis_at))
    return factor_of


def bell_draw(rng, shape, width, reach, cuts=(), held_as=jnp.bfloat16):
    gain = levels(rng, shape, cuts, -0.22, 0.18) if cuts else 1.0
    drawn = jax.random.normal(rng, shape, jnp.float32) * width * gain
    return jnp.minimum(jnp.maximum(drawn, -reach), reach).astype(held_as)


def setup_inputs(seed: int = 0, part: int = 0) -> dict:
    arg_keys = jax.random.split(jax.random.key(seed), 8)
    part_splits = jax.random.split(jax.random.fold_in(arg_keys[7], part), 8)
    query_grads = bell_draw(arg_keys[0], (MODULES, QUERIES, DIM, DIM), 0.03125, 0.1875, ((2, 16),), jnp.float32)
    train_grads = bell_draw(part_splits[1], (TOTAL_SLOT_ROWS, EXAMPLES, DIM, DIM), 0.03125, 0.1875, ((0, 16),), jnp.float32)
    out_basis = bell_draw(arg_keys[2], (TOTAL_SLOT_ROWS, DIM, DIM), DIM ** -0.5, 0.5, ((0, 16),), jnp.float32)
    in_basis = bell_draw(arg_keys[3], (TOTAL_SLOT_ROWS, DIM, DIM), DIM ** -0.5, 0.5, ((0, 16),), jnp.float32)
    corrections = jnp.clip(jnp.exp(math.log(10.0) - 6.9077553 * jax.random.uniform(arg_keys[4], (TOTAL_SLOT_ROWS, DIM, DIM), jnp.float32) ** levels(arg_keys[4], (TOTAL_SLOT_ROWS, DIM, DIM), ((0, 16),), -0.2, 0.2)), 0.01, 10.0)
    ranks = set_ends(jax.random.randint(arg_keys[5], (MODULES,), DIM // 4, DIM + 1), jax.random.fold_in(arg_keys[5], 1), DIM // 4, DIM).astype(jnp.int32)
    slot_modules = draw_slot_modules(jax.random.fold_in(arg_keys[7], 71), part)
    return dict(query_grads=query_grads, train_grads=train_grads, out_basis=out_basis, in_basis=in_basis, corrections=corrections, ranks=ranks, slot_modules=slot_modules)


def rotate(field, output_eigenbasis, inner_basis):
    inner = jnp.einsum('noi,ib->nob', field, inner_basis, precision=lax.Precision.HIGHEST)
    return jnp.einsum('oa,nob->nab', output_eigenbasis, inner, precision=lax.Precision.HIGHEST)


def slot_weight(spectrum, keep_rank):
    damping = 0.1 * jnp.mean(spectrum)
    positions = jnp.arange(spectrum.shape[0]).astype(jnp.int32)
    kept_mask = (positions[:, None] < keep_rank) & (positions[None, :] < keep_rank)
    return jnp.where(kept_mask, 1.0 / (spectrum + damping), jnp.zeros_like(spectrum))


def reference(query_grads, train_grads, out_basis, in_basis, corrections, ranks, slot_modules):
    def per_slot(running, inputs):
        module, train_block, output_eigenbasis, inner_basis, spectrum = inputs
        safe_index = jnp.maximum(module, 0)

        def occupied(unused):
            weight = slot_weight(spectrum, ranks[safe_index])
            scaled = rotate(query_grads[safe_index], output_eigenbasis, inner_basis) * weight
            rotated = rotate(train_block, output_eigenbasis, inner_basis)
            return jnp.einsum('qab,eab->qe', scaled, rotated, precision=lax.Precision.HIGHEST)

        def vacant(unused):
            return jnp.zeros((QUERIES, EXAMPLES), jnp.float32)

        return running + lax.cond(module >= 0, occupied, vacant, 0), None

    start = jnp.zeros((QUERIES, EXAMPLES), jnp.float32)
    running, unused = lax.scan(per_slot, start, (slot_modules, train_grads, out_basis, in_basis, corrections))
    return running
```

```python
import functools
import jax
import jax.numpy as jnp
from jax import lax
from jax.experimental import pallas as pl
from jax.experimental.pallas import tpu as pltpu
from jax.sharding import PartitionSpec as P

F32 = jnp.float32
BF16 = jnp.bfloat16
NT = (((1,), (1,)), ((), ()))
NN = (((1,), (0,)), ((), ()))


def entry_slot(slots, owner, core, entry):
    probe = slots[2 * owner + core]
    return jnp.where(probe < 0, 1 - entry, entry)


def chip_list(slots, chip, cap):
    found = []
    for core in range(2):
        owner = chip * 2 + core
        found.append([slots[2 * owner + entry_slot(slots, owner, core, e)] for e in range(2)])
    if cap == 4:
        return found[0] + found[1]
    return [found[0][0], jnp.maximum(found[0][1], found[1][0]), found[1][1]]


def split(x):
    high = x.astype(BF16)
    return high, (x - high.astype(F32)).astype(BF16)


def pack_kernel(chips, cap, share, slots, place, query, own, *sends):
    chip, group = place[0], place[2]
    rows = query.shape[2]
    for k, module in enumerate(chip_list(slots, chip, cap)):
        module = jnp.maximum(module, 0)
        for r in range(rows):
            own[k, r] = query[module, :, r, :]
    start = pl.multiple_of(group * share, share)
    for d in range(1, chips):
        for k, module in enumerate(chip_list(slots, chip ^ d, cap)):
            module = jnp.maximum(module, 0)
            for r in range(rows):
                sends[d - 1][k, r] = query[module, pl.ds(start, share), r, :]


def pack(chips, cap, share, slots, place, query):
    _, count, rows, width = query.shape
    vmem = pl.BlockSpec(memory_space=pltpu.VMEM)
    return pl.pallas_call(
        functools.partial(pack_kernel, chips, cap, share),
        grid_spec=pltpu.PrefetchScalarGridSpec(
            num_scalar_prefetch=2,
            grid=(),
            in_specs=[vmem],
            out_specs=[vmem] * chips,
        ),
        out_shape=[jax.ShapeDtypeStruct((cap, rows, count, width), F32)]
        + [jax.ShapeDtypeStruct((cap, rows, share, width), F32)] * (chips - 1),
        cost_estimate=pl.CostEstimate(flops=0, bytes_accessed=2 * query.size * 4, transcendentals=0),
        name="pack",
    )(slots, place, query)


def fold_kernel(chips, slots, place, ranks, train, out_basis, in_basis, corrections, mine, other,
                w_in, w_out, w_out_t, w_in_t, weight, turned):
    core = place[1]
    owner = place[0] * 2 + core
    entry = pl.program_id(0)
    block, dim = train.shape[1], train.shape[2]
    rows = dim // (2 * chips)

    @pl.when(pl.program_id(1) == 0)
    def _():
        module = slots[2 * owner + entry_slot(slots, owner, core, entry)]
        rank = jnp.where(module >= 0, ranks[jnp.maximum(module, 0)], 0)
        spectrum = corrections[0]
        damping = 0.1 * (jnp.sum(spectrum) / (dim * dim))
        a = lax.broadcasted_iota(jnp.int32, (dim, dim), 0)
        b = lax.broadcasted_iota(jnp.int32, (dim, dim), 1)
        kept = jnp.where((a < rank) & (b < rank), 1.0 / (spectrum + damping), 0.0)
        weight[...] = kept.T
        for ref, value in ((w_in, in_basis[0]), (w_out, out_basis[0]),
                           (w_out_t, out_basis[0].T), (w_in_t, in_basis[0].T)):
            high, low = split(value)
            both = jnp.concatenate([high, low], axis=1)
            ref[...] = jnp.concatenate([both, both], axis=0)

    def times(x, ref):
        flat = x.reshape(block * dim, dim)
        high, low = split(flat)
        product = lax.dot_general(jnp.concatenate([high, low], axis=1), ref[...], NN, preferred_element_type=F32)
        return (product[:, :dim] + product[:, dim:]).reshape(block, dim, dim)

    x = times(train[0], w_in)
    x = times(jnp.swapaxes(x, 1, 2), w_out) * weight[...][None]
    x = jnp.swapaxes(times(x, w_out_t), 1, 2)
    turned[...] = times(x, w_in_t).reshape(block * dim, dim)
    for chip in range(chips):
        for r in range(rows):
            here = (chip * 2 + core) * rows + r
            there = (chip * 2 + 1 - core) * rows + r
            mine[0, chip, r] = turned[pl.ds(here, block, stride=dim), :]
            other[0, chip, r] = turned[pl.ds(there, block, stride=dim), :]


def fold(chips, part, parts, slots, place, ranks, train, out_basis, in_basis, corrections):
    entries, examples, dim, _ = train.shape
    rows = dim // (2 * chips)
    block = 8
    size = examples // parts
    steps = size // block

    def slot_of(entry, slots, place):
        return entry_slot(slots, place[0] * 2 + place[1], place[1], entry)

    square = pl.BlockSpec((1, dim, dim), lambda n, b, s, p, r: (slot_of(n, s, p), 0, 0))
    out = pl.BlockSpec((1, chips, rows, block, dim), lambda n, b, s, p, r: (n, 0, 0, b, 0))
    shape = jax.ShapeDtypeStruct((entries, chips, rows, size, dim), F32)
    double = pltpu.VMEM((2 * dim, 2 * dim), BF16)
    return pl.pallas_call(
        functools.partial(fold_kernel, chips),
        grid_spec=pltpu.PrefetchScalarGridSpec(
            num_scalar_prefetch=3,
            grid=(entries, steps),
            in_specs=[pl.BlockSpec((1, block, dim, dim), lambda n, b, s, p, r: (slot_of(n, s, p), part * steps + b, 0, 0)),
                      square, square, square],
            out_specs=[out, out],
            scratch_shapes=[double] * 4 + [pltpu.VMEM((dim, dim), F32), pltpu.VMEM((block * dim, dim), F32)],
        ),
        out_shape=[shape, shape],
        compiler_params=pltpu.CompilerParams(vmem_limit_bytes=48 << 20),
        cost_estimate=pl.CostEstimate(flops=entries * size * 8 * dim**3 * 4, bytes_accessed=entries * size * dim * dim * 8, transcendentals=0),
        name="fold",
    )(slots, place, ranks, train, out_basis, in_basis, corrections)


def score_kernel(cap, shifts, groups, share, parts, place, *refs):
    core, group = place[1], place[2]
    refs = list(refs)
    previous, out = refs.pop(0), refs.pop()
    total = None
    for d in shifts:
        if d == 0:
            own = refs.pop(0)
            queries = [own.at[:, :, pl.ds(pl.multiple_of((group ^ t) * share, share), share), :] for t in range(groups)]
        else:
            queries = [refs.pop(0) for _ in range(groups)]
        folded = [[refs.pop(0) for _ in range(parts)] for _ in range(2)]
        rows = folded[0][0].shape[2]
        for side in range(2):
            for entry in range(2):
                position = jnp.where(core == side, 0, cap - 2) + entry
                high, low = split(jnp.concatenate(
                    [jnp.concatenate([q[position, r] for q in queries], axis=0) for r in range(rows)], axis=1))
                left = jnp.concatenate([high, low], axis=0)
                high, low = split(jnp.concatenate(
                    [jnp.concatenate([g[entry, 0, r] for g in folded[side]], axis=0) for r in range(rows)], axis=1))
                right = jnp.concatenate([high, low], axis=0)
                product = lax.dot_general(left, right, NT, preferred_element_type=F32)
                total = product if total is None else total + product
    half, examples = total.shape[0] // 2, total.shape[1] // 2
    result = (total[:half, :examples] + total[half:, examples:]) + (total[:half, examples:] + total[half:, :examples])
    out[...] = result + previous[...]


def score(cap, shifts, groups, share, place, previous, queries, folded):
    parts = len(folded[0])
    vmem = pl.BlockSpec(memory_space=pltpu.VMEM)
    operands, specs = [previous], [vmem]
    for d, query in zip(shifts, queries):
        operands += query
        specs += [vmem] * len(query)
        for side in folded:
            for g in side:
                operands.append(g)
                specs.append(pl.BlockSpec((g.shape[0], 1) + g.shape[2:], lambda n, p, d=d: (0, p[0] ^ d, 0, 0, 0)))
    return pl.pallas_call(
        functools.partial(score_kernel, cap, shifts, groups, share, parts),
        grid_spec=pltpu.PrefetchScalarGridSpec(
            num_scalar_prefetch=1, grid=(1,), in_specs=specs, out_specs=vmem),
        out_shape=jax.ShapeDtypeStruct(previous.shape, F32),
        compiler_params=pltpu.CompilerParams(vmem_limit_bytes=48 << 20),
        cost_estimate=pl.CostEstimate(flops=len(shifts) * 4 * 2 * 64 * 128 * 1024, bytes_accessed=len(shifts) * 1536 * 1024, transcendentals=0),
        name="score",
    )(place, *operands)


def order_of(chips):
    return sorted(range(1, chips), key=lambda d: (d.bit_length() > 2, -d if d.bit_length() > 2 else d))


def body(devices, groups, query_grads, train_grads, out_basis, in_basis, corrections, ranks, slot_modules):
    chips, cap, parts = devices // 2, 4, 4
    count, examples = query_grads.shape[1], train_grads.shape[1]
    share = count // groups
    index, group = lax.axis_index("module"), lax.axis_index("group")
    place = jnp.stack([index // 2, index % 2, group]).astype(jnp.int32)
    own, *sends = pack(chips, cap, share, slot_modules, place, query_grads)
    order = order_of(chips)
    arrived = {0: [own]}
    for d in order:
        direct = lax.ppermute(sends[d - 1], "module", [(i, i ^ (2 * d)) for i in range(devices)])
        arrived[d] = [direct]
        for t in range(1, groups):
            arrived[d].append(lax.ppermute(direct, "group", [(i, i ^ t) for i in range(groups)]))
    mine, other = [], []
    for part in range(parts):
        here, there = fold(chips, part, parts, slot_modules, place, ranks, train_grads, out_basis, in_basis, corrections)
        mine.append(here)
        other.append(lax.ppermute(there, "module", [(i, i ^ 1) for i in range(devices)]))
    total = jnp.zeros((count, examples), F32)
    everything = [0] + order
    step = max(len(everything) // 4, 1)
    for first in range(0, len(everything), step):
        shifts = tuple(everything[first:first + step])
        total = score(cap, shifts, groups, share, place, total, [arrived[d] for d in shifts], [mine, other])
    blocks = total.reshape(groups, share, examples)
    total = blocks[jnp.arange(groups) ^ group].reshape(count, examples)
    stride = 1
    while stride < devices:
        total = total + lax.ppermute(total, "module", [(i, i ^ stride) for i in range(devices)])
        stride *= 2
    return total


def solution(mesh):
    devices, groups = mesh.shape["module"], mesh.shape["group"]

    def whole(*arrays):
        return body(devices, groups, *arrays)

    return jax.shard_map(
        whole,
        mesh=mesh,
        in_specs=(
            P(None, None, "module", None),
            P("module", "group", None, None),
            P("module", None, None),
            P("module", None, None),
            P("module", None, None),
            P(),
            P(),
        ),
        out_specs=P(None, "group"),
        check_vma=False,
    )
```

```python
import functools
import jax
import jax.numpy as jnp
from jax import lax
from jax.experimental import pallas as pl
from jax.experimental.pallas import tpu as pltpu
from jax.sharding import PartitionSpec as P

F32 = jnp.float32
BF16 = jnp.bfloat16
SUB = 8
START = (6, 1, 2, 3, 7, 4, 5)
USE = (1, 6, 2, 3, 7, 4, 5)
BLOCK = 16
NT = (((1,), (1,)), ((), ()))
NN = (((1,), (0,)), ((), ()))


def entry_slot(slots, owner, core, entry):
    probe = slots[2 * owner + core]
    return jnp.where(probe < 0, 1 - entry, entry)


def chip_list(slots, chip, cap):
    found = []
    for core in range(2):
        owner = chip * 2 + core
        found.append([slots[2 * owner + entry_slot(slots, owner, core, e)] for e in range(2)])
    if cap == 4:
        return found[0] + found[1]
    return [found[0][0], jnp.maximum(found[0][1], found[1][0]), found[1][1]]


def split(x):
    high = x.astype(BF16)
    return high, (x - high.astype(F32)).astype(BF16)


def pack_kernel(chips, cap, share, slots, place, query, own, *rest):
    sends, sem = rest[:-1], rest[-1]
    chip, group = place[0], place[2]
    start = pl.multiple_of(group * share, share)
    copies = []
    for d in range(1, chips):
        for k, module in enumerate(chip_list(slots, chip ^ d, cap)):
            source = query.at[jnp.maximum(module, 0), pl.ds(start, share)]
            copies.append(pltpu.make_async_copy(source, sends[d - 1].at[k], sem))
    for k, module in enumerate(chip_list(slots, chip, cap)):
        copies.append(pltpu.make_async_copy(query.at[jnp.maximum(module, 0)], own.at[k], sem))
    for copy in copies:
        copy.start()
    for copy in copies:
        copy.wait()


def pack(chips, cap, share, slots, place, query):
    _, count, rows, width = query.shape
    vmem = pl.BlockSpec(memory_space=pltpu.VMEM)
    return pl.pallas_call(
        functools.partial(pack_kernel, chips, cap, share),
        grid_spec=pltpu.PrefetchScalarGridSpec(
            num_scalar_prefetch=2,
            grid=(),
            in_specs=[pl.BlockSpec(memory_space=pltpu.HBM)],
            out_specs=[vmem] * chips,
            scratch_shapes=[pltpu.SemaphoreType.DMA],
        ),
        out_shape=[jax.ShapeDtypeStruct((cap, count, rows, width), F32)]
        + [jax.ShapeDtypeStruct((cap, share, rows, width), F32)] * (chips - 1),
        compiler_params=pltpu.CompilerParams(vmem_limit_bytes=8 << 20),
        cost_estimate=pl.CostEstimate(flops=0, bytes_accessed=2 * query.size * 4, transcendentals=0),
        name="pack",
    )(slots, place, query)


def fold_kernel(chips, slots, place, ranks, train, out_basis, in_basis, corrections, mine, other,
                w_in, w_out, w_out_t, w_in_t, weight):
    core = place[1]
    owner = place[0] * 2 + core
    entry = pl.program_id(0)
    block, dim = train.shape[1], train.shape[2]
    rows = dim // (2 * chips)

    @pl.when(pl.program_id(1) == 0)
    def _():
        module = slots[2 * owner + entry_slot(slots, owner, core, entry)]
        rank = jnp.where(module >= 0, ranks[jnp.maximum(module, 0)], 0)
        spectrum = corrections[0]
        damping = 0.1 * (jnp.sum(spectrum) / (dim * dim))
        a = lax.broadcasted_iota(jnp.int32, (dim, dim), 0)
        b = lax.broadcasted_iota(jnp.int32, (dim, dim), 1)
        kept = jnp.where((a < rank) & (b < rank), 1.0 / (spectrum + damping), 0.0)
        weight[...] = kept.T
        for ref, value in ((w_in, in_basis[0]), (w_out, out_basis[0]),
                           (w_out_t, out_basis[0].T), (w_in_t, in_basis[0].T)):
            high, low = split(value)
            both = jnp.concatenate([high, low], axis=1)
            ref[...] = jnp.concatenate([both, both], axis=0)

    def times(x, ref):
        flat = x.reshape(SUB * dim, dim)
        high, low = split(flat)
        product = lax.dot_general(jnp.concatenate([high, low], axis=1), ref[...], NN, preferred_element_type=F32)
        return (product[:, :dim] + product[:, dim:]).reshape(SUB, dim, dim)

    def chain(sub):
        x = times(train[0, sub * SUB:(sub + 1) * SUB], w_in)
        x = times(jnp.swapaxes(x, 1, 2), w_out) * weight[...][None]
        x = jnp.swapaxes(times(x, w_out_t), 1, 2)
        x = jnp.swapaxes(times(x, w_in_t), 0, 1).reshape(chips, 2, rows, SUB, dim)
        place_in = slice(sub * SUB, (sub + 1) * SUB)
        first = core == 0
        mine[0, :, :, place_in] = jnp.where(first, x[:, 0], x[:, 1])
        other[0, :, :, place_in] = jnp.where(first, x[:, 1], x[:, 0])

    for sub in range(block // SUB):
        chain(sub)


def fold(chips, part, parts, slots, place, ranks, train, out_basis, in_basis, corrections):
    entries, examples, dim, _ = train.shape
    rows = dim // (2 * chips)
    size = examples // parts
    block = min(size, BLOCK)
    steps = size // block

    def slot_of(entry, slots, place):
        return entry_slot(slots, place[0] * 2 + place[1], place[1], entry)

    square = pl.BlockSpec((1, dim, dim), lambda n, b, s, p, r: (slot_of(n, s, p), 0, 0))
    out = pl.BlockSpec((1, chips, rows, block, dim), lambda n, b, s, p, r: (n, 0, 0, b, 0))
    shape = jax.ShapeDtypeStruct((entries, chips, rows, size, dim), F32)
    double = pltpu.VMEM((2 * dim, 2 * dim), BF16)
    return pl.pallas_call(
        functools.partial(fold_kernel, chips),
        grid_spec=pltpu.PrefetchScalarGridSpec(
            num_scalar_prefetch=3,
            grid=(entries, steps),
            in_specs=[pl.BlockSpec((1, block, dim, dim), lambda n, b, s, p, r: (slot_of(n, s, p), part * steps + b, 0, 0)),
                      square, square, square],
            out_specs=[out, out],
            scratch_shapes=[double] * 4 + [pltpu.VMEM((dim, dim), F32)],
        ),
        out_shape=[shape, shape],
        compiler_params=pltpu.CompilerParams(vmem_limit_bytes=24 << 20),
        cost_estimate=pl.CostEstimate(flops=entries * size * 8 * dim**3 * 4, bytes_accessed=entries * size * dim * dim * 8, transcendentals=0),
        name="fold",
    )(slots, place, ranks, train, out_basis, in_basis, corrections)


def score_kernel(cap, shifts, groups, share, parts, place, *refs):
    chip, core, group = place[0], place[1], place[2]
    refs = list(refs)
    out = refs.pop()
    previous = refs.pop(0)
    folded = [[refs.pop(0) for _ in range(parts)] for _ in range(2)]
    rows = folded[0][0].shape[2]
    total = None
    for d in shifts:
        if d == 0:
            own = refs.pop(0)
            queries = [own.at[:, pl.ds(pl.multiple_of((group ^ t) * share, share), share)] for t in range(groups)]
        else:
            queries = [refs.pop(0) for _ in range(groups)]
        for side in range(2):
            for entry in range(2):
                position = jnp.where(core == side, 0, cap - 2) + entry
                high, low = split(jnp.concatenate(
                    [jnp.concatenate([q[position, :, r, :] for q in queries], axis=0) for r in range(rows)], axis=1))
                left = jnp.concatenate([high, low], axis=0)
                high, low = split(jnp.concatenate(
                    [jnp.concatenate([g[entry, chip ^ d, r] for g in folded[side]], axis=0) for r in range(rows)], axis=1))
                right = jnp.concatenate([high, low], axis=0)
                product = lax.dot_general(left, right, NT, preferred_element_type=F32)
                total = product if total is None else total + product
    half, examples = total.shape[0] // 2, total.shape[1] // 2
    result = (total[:half, :examples] + total[half:, examples:]) + (total[:half, examples:] + total[half:, :examples])
    for t in range(groups):
        place_out = pl.ds(pl.multiple_of((group ^ t) * share, share), share)
        out[place_out, :] = result[t * share:(t + 1) * share] + previous[place_out, :]


def score(cap, shifts, groups, share, place, previous, queries, folded):
    parts = len(folded[0])
    vmem = pl.BlockSpec(memory_space=pltpu.VMEM)
    operands = [previous] + folded[0] + folded[1]
    for query in queries:
        operands += query
    return pl.pallas_call(
        functools.partial(score_kernel, cap, shifts, groups, share, parts),
        grid_spec=pltpu.PrefetchScalarGridSpec(
            num_scalar_prefetch=1, grid=(), in_specs=[vmem] * len(operands), out_specs=vmem),
        out_shape=jax.ShapeDtypeStruct(previous.shape, F32),
        compiler_params=pltpu.CompilerParams(vmem_limit_bytes=40 << 20),
        cost_estimate=pl.CostEstimate(flops=len(shifts) * 4 * 2 * 64 * 128 * 1024, bytes_accessed=len(shifts) * 1536 * 1024, transcendentals=0),
        name="score",
    )(place, *operands)


def order_of(chips):
    if chips == 8:
        return START, USE
    return (tuple(range(1, chips)),) * 2


def body(devices, groups, cap, query_grads, train_grads, out_basis, in_basis, corrections, ranks, slot_modules):
    chips, parts = devices // 2, 4
    count, examples = query_grads.shape[1], train_grads.shape[1]
    share = count // groups
    index, group = lax.axis_index("module"), lax.axis_index("group")
    place = jnp.stack([index // 2, index % 2, group]).astype(jnp.int32)
    own, *sends = pack(chips, cap, share, slot_modules, place, query_grads)
    start, use = order_of(chips)
    arrived = {0: [own]}
    for d in start:
        arrived[d] = [lax.ppermute(sends[d - 1], "module", [(i, i ^ (2 * d)) for i in range(devices)])]
    for d in use:
        for t in range(1, groups):
            arrived[d].append(lax.ppermute(arrived[d][0], "group", [(i, i ^ t) for i in range(groups)]))
    mine, other = [], []
    for part in range(parts):
        here, there = fold(chips, part, parts, slot_modules, place, ranks, train_grads, out_basis, in_basis, corrections)
        mine.append(here)
        other.append(lax.ppermute(there, "module", [(i, i ^ 1) for i in range(devices)]))
    total = jnp.zeros((count, examples), F32)
    everything = (0,) + use
    cuts = [0, *range(len(everything) - 1, 0, -2)[::-1], len(everything)]
    for first, last in zip(cuts, cuts[1:]):
        shifts = everything[first:last]
        total = score(cap, shifts, groups, share, place, total, [arrived[d] for d in shifts], [mine, other])
    stride = 1
    while stride < devices:
        total = total + lax.ppermute(total, "module", [(i, i ^ stride) for i in range(devices)])
        stride *= 2
    return total


def solution(mesh):
    devices, groups = mesh.shape["module"], mesh.shape["group"]

    def branch(cap, *arrays):
        return body(devices, groups, cap, *arrays)

    def whole(*arrays):
        if devices != 16:
            return branch(4, *arrays)
        fullest = jnp.min(arrays[-1].reshape(-1, 4), axis=1)
        return lax.cond(jnp.max(fullest) < 0, functools.partial(branch, 3), functools.partial(branch, 4), *arrays)

    return jax.shard_map(
        whole,
        mesh=mesh,
        in_specs=(
            P(None, None, "module", None),
            P("module", "group", None, None),
            P("module", None, None),
            P("module", None, None),
            P("module", None, None),
            P(),
            P(),
        ),
        out_specs=P(None, "group"),
        check_vma=False,
    )
```

```python
import functools
import jax
import jax.numpy as jnp
from jax import lax
from jax.experimental import pallas as pl
from jax.experimental.pallas import tpu as pltpu
from jax.sharding import PartitionSpec as P

F32 = jnp.float32
BF16 = jnp.bfloat16
SUB = 8
START = (6, 1, 2, 3, 7, 4, 5)
USE = (1, 6, 2, 3, 7, 4, 5)
BLOCK = 16
NT = (((1,), (1,)), ((), ()))
NN = (((1,), (0,)), ((), ()))


def entry_slot(slots, owner, core, entry):
    probe = slots[2 * owner + core]
    return jnp.where(probe < 0, 1 - entry, entry)


def chip_list(slots, chip, cap):
    found = []
    for core in range(2):
        owner = chip * 2 + core
        found.append([slots[2 * owner + entry_slot(slots, owner, core, e)] for e in range(2)])
    if cap == 4:
        return found[0] + found[1]
    return [found[0][0], jnp.maximum(found[0][1], found[1][0]), found[1][1]]


def tail_of():
    return 0


def split(x):
    high = x.astype(BF16)
    return high, (x - high.astype(F32)).astype(BF16)


def pack_kernel(chips, cap, share, slots, place, query, own, *rest):
    sends, sem = rest[:-1], rest[-1]
    chip, group = place[0], place[2]
    start = pl.multiple_of(group * share, share)
    tail = tail_of()
    half = share // 2
    copies = []
    for d in range(1, chips):
        for k, module in enumerate(chip_list(slots, chip ^ d, cap)):
            source = query.at[jnp.maximum(module, 0)]
            if d != tail:
                copies.append(pltpu.make_async_copy(source.at[pl.ds(start, share)], sends[d - 1].at[k], sem))
                continue
            copies.append(pltpu.make_async_copy(source.at[pl.ds(start, half)], sends[d - 1].at[k], sem))
            for t in range(2):
                late = pl.multiple_of((group ^ t) * share + half, half)
                copies.append(pltpu.make_async_copy(
                    source.at[pl.ds(late, half)], sends[chips - 1].at[k, pl.ds(t * half, half)], sem))
    for k, module in enumerate(chip_list(slots, chip, cap)):
        copies.append(pltpu.make_async_copy(query.at[jnp.maximum(module, 0)], own.at[k], sem))
    for copy in copies:
        copy.start()
    for copy in copies:
        copy.wait()


def pack(chips, cap, share, slots, place, query):
    _, count, rows, width = query.shape
    vmem = pl.BlockSpec(memory_space=pltpu.VMEM)
    tail = tail_of()
    sizes = [count] + [share // 2 if d == tail else share for d in range(1, chips)] + [share] * (tail > 0)
    return pl.pallas_call(
        functools.partial(pack_kernel, chips, cap, share),
        grid_spec=pltpu.PrefetchScalarGridSpec(
            num_scalar_prefetch=2,
            grid=(),
            in_specs=[pl.BlockSpec(memory_space=pltpu.HBM)],
            out_specs=[vmem] * len(sizes),
            scratch_shapes=[pltpu.SemaphoreType.DMA],
        ),
        out_shape=[jax.ShapeDtypeStruct((cap, size, rows, width), F32) for size in sizes],
        compiler_params=pltpu.CompilerParams(vmem_limit_bytes=8 << 20),
        cost_estimate=pl.CostEstimate(flops=0, bytes_accessed=2 * query.size * 4, transcendentals=0),
        name="pack",
    )(slots, place, query)


def fold_kernel(chips, slots, place, ranks, train, out_basis, in_basis, corrections, mine, other,
                w_in, w_out, w_out_t, w_in_t, weight):
    core = place[1]
    owner = place[0] * 2 + core
    entry = pl.program_id(0)
    block, dim = train.shape[1], train.shape[2]
    rows = dim // (2 * chips)

    @pl.when(pl.program_id(1) == 0)
    def _():
        module = slots[2 * owner + entry_slot(slots, owner, core, entry)]
        rank = jnp.where(module >= 0, ranks[jnp.maximum(module, 0)], 0)
        spectrum = corrections[0]
        damping = 0.1 * (jnp.sum(spectrum) / (dim * dim))
        a = lax.broadcasted_iota(jnp.int32, (dim, dim), 0)
        b = lax.broadcasted_iota(jnp.int32, (dim, dim), 1)
        kept = jnp.where((a < rank) & (b < rank), 1.0 / (spectrum + damping), 0.0)
        weight[...] = kept.T
        for ref, value in ((w_in, in_basis[0]), (w_out, out_basis[0]),
                           (w_out_t, out_basis[0].T), (w_in_t, in_basis[0].T)):
            high, low = split(value)
            both = jnp.concatenate([high, low], axis=1)
            ref[...] = jnp.concatenate([both, both], axis=0)

    def times(x, ref):
        flat = x.reshape(SUB * dim, dim)
        high, low = split(flat)
        product = lax.dot_general(jnp.concatenate([high, low], axis=1), ref[...], NN, preferred_element_type=F32)
        return (product[:, :dim] + product[:, dim:]).reshape(SUB, dim, dim)

    def chain(sub):
        x = times(train[0, sub * SUB:(sub + 1) * SUB], w_in)
        x = times(jnp.swapaxes(x, 1, 2), w_out) * weight[...][None]
        x = jnp.swapaxes(times(x, w_out_t), 1, 2)
        x = jnp.swapaxes(times(x, w_in_t), 0, 1).reshape(chips, 2, rows, SUB, dim)
        place_in = slice(sub * SUB, (sub + 1) * SUB)
        first = core == 0
        mine[0, :, :, place_in] = jnp.where(first, x[:, 0], x[:, 1])
        other[0, :, :, place_in] = jnp.where(first, x[:, 1], x[:, 0])

    for sub in range(block // SUB):
        chain(sub)


def fold(chips, part, parts, slots, place, ranks, train, out_basis, in_basis, corrections):
    entries, examples, dim, _ = train.shape
    rows = dim // (2 * chips)
    size = examples // parts
    block = min(size, BLOCK)
    steps = size // block

    def slot_of(entry, slots, place):
        return entry_slot(slots, place[0] * 2 + place[1], place[1], entry)

    square = pl.BlockSpec((1, dim, dim), lambda n, b, s, p, r: (slot_of(n, s, p), 0, 0))
    out = pl.BlockSpec((1, chips, rows, block, dim), lambda n, b, s, p, r: (n, 0, 0, b, 0))
    shape = jax.ShapeDtypeStruct((entries, chips, rows, size, dim), F32)
    double = pltpu.VMEM((2 * dim, 2 * dim), BF16)
    return pl.pallas_call(
        functools.partial(fold_kernel, chips),
        grid_spec=pltpu.PrefetchScalarGridSpec(
            num_scalar_prefetch=3,
            grid=(entries, steps),
            in_specs=[pl.BlockSpec((1, block, dim, dim), lambda n, b, s, p, r: (slot_of(n, s, p), part * steps + b, 0, 0)),
                      square, square, square],
            out_specs=[out, out],
            scratch_shapes=[double] * 4 + [pltpu.VMEM((dim, dim), F32)],
        ),
        out_shape=[shape, shape],
        compiler_params=pltpu.CompilerParams(vmem_limit_bytes=24 << 20),
        cost_estimate=pl.CostEstimate(flops=entries * size * 8 * dim**3 * 4, bytes_accessed=entries * size * dim * dim * 8, transcendentals=0),
        name="fold",
    )(slots, place, ranks, train, out_basis, in_basis, corrections)


def score_kernel(cap, shifts, groups, share, parts, place, *refs):
    chip, core, group = place[0], place[1], place[2]
    refs = list(refs)
    out = refs.pop()
    previous = refs.pop(0)
    folded = [[refs.pop(0) for _ in range(parts)] for _ in range(2)]
    rows = folded[0][0].shape[2]
    total = None
    for d in shifts:
        if d == 0:
            own = refs.pop(0)
            queries = [own.at[:, pl.ds(pl.multiple_of((group ^ t) * share, share), share)] for t in range(groups)]
        else:
            queries = [refs.pop(0) for _ in range(groups)]
        late = refs.pop(0) if d and d == tail_of() else None

        def query_rows(position, r):
            found = []
            for t, q in enumerate(queries):
                found.append(q[position, :, r, :])
                if late is not None:
                    found.append(late[position, t * (share // 2):(t + 1) * (share // 2), r, :])
            return jnp.concatenate(found, axis=0)

        def grads(side, entry):
            return jnp.concatenate(
                [jnp.concatenate([g[entry, chip ^ d, r] for g in folded[side]], axis=0) for r in range(rows)], axis=1)

        if cap == 4:
            work = [(core * 2, grads(0, 0)), (core * 2 + 1, grads(0, 1)),
                    (2 - core * 2, grads(1, 0)), (3 - core * 2, grads(1, 1))]
        else:
            work = [(core * 2, grads(0, core)), (1, grads(0, 1 - core) + grads(1, core)), (2 - core * 2, grads(1, 1 - core))]
        for position, block in work:
            high, low = split(jnp.concatenate([query_rows(position, r) for r in range(rows)], axis=1))
            left = jnp.concatenate([high, low], axis=0)
            high, low = split(block)
            right = jnp.concatenate([high, low], axis=0)
            product = lax.dot_general(left, right, NT, preferred_element_type=F32)
            total = product if total is None else total + product
    half, examples = total.shape[0] // 2, total.shape[1] // 2
    result = (total[:half, :examples] + total[half:, examples:]) + (total[:half, examples:] + total[half:, :examples])
    for t in range(groups):
        place_out = pl.ds(pl.multiple_of((group ^ t) * share, share), share)
        out[place_out, :] = result[t * share:(t + 1) * share] + previous[place_out, :]


def score(cap, shifts, groups, share, place, previous, queries, folded):
    parts = len(folded[0])
    vmem = pl.BlockSpec(memory_space=pltpu.VMEM)
    operands = [previous] + folded[0] + folded[1]
    for query in queries:
        operands += query
    return pl.pallas_call(
        functools.partial(score_kernel, cap, shifts, groups, share, parts),
        grid_spec=pltpu.PrefetchScalarGridSpec(
            num_scalar_prefetch=1, grid=(), in_specs=[vmem] * len(operands), out_specs=vmem),
        out_shape=jax.ShapeDtypeStruct(previous.shape, F32),
        compiler_params=pltpu.CompilerParams(vmem_limit_bytes=40 << 20),
        cost_estimate=pl.CostEstimate(flops=len(shifts) * 4 * 2 * 64 * 128 * 1024, bytes_accessed=len(shifts) * 1536 * 1024, transcendentals=0),
        name="score",
    )(place, *operands)


def order_of(chips):
    if chips == 8:
        return START, USE
    return (tuple(range(1, chips)),) * 2


def body(devices, groups, cap, query_grads, train_grads, out_basis, in_basis, corrections, ranks, slot_modules):
    chips, parts = devices // 2, 4
    count, examples = query_grads.shape[1], train_grads.shape[1]
    share = count // groups
    index, group = lax.axis_index("module"), lax.axis_index("group")
    place = jnp.stack([index // 2, index % 2, group]).astype(jnp.int32)
    own, *sends = pack(chips, cap, share, slot_modules, place, query_grads)
    start, use = order_of(chips)
    arrived = {0: [own]}
    for d in start:
        arrived[d] = [lax.ppermute(sends[d - 1], "module", [(i, i ^ (2 * d)) for i in range(devices)])]
    tail = tail_of()
    if tail:
        late = lax.ppermute(sends[-1], "module", [(i, i ^ (2 * tail)) for i in range(devices)])
    for d in use:
        for t in range(1, groups):
            arrived[d].append(lax.ppermute(arrived[d][0], "group", [(i, i ^ t) for i in range(groups)]))
    if tail:
        arrived[tail].append(late)
    mine, other = [], []
    for part in range(parts):
        here, there = fold(chips, part, parts, slot_modules, place, ranks, train_grads, out_basis, in_basis, corrections)
        mine.append(here)
        other.append(lax.ppermute(there, "module", [(i, i ^ 1) for i in range(devices)]))
    total = jnp.zeros((count, examples), F32)
    everything = (0,) + use
    cuts = [0, *range(len(everything) - 1, 0, -2)[::-1], len(everything)]
    for first, last in zip(cuts, cuts[1:]):
        shifts = everything[first:last]
        total = score(cap, shifts, groups, share, place, total, [arrived[d] for d in shifts], [mine, other])
    stride = 1
    while stride < devices:
        radix = 4 if 1 < stride and stride * 2 < devices else 2
        total += sum(lax.ppermute(total, "module", [(i, i ^ (stride * t)) for i in range(devices)]) for t in range(1, radix))
        stride *= radix
    return total


def solution(mesh):
    devices, groups = mesh.shape["module"], mesh.shape["group"]

    def branch(cap, *arrays):
        return body(devices, groups, cap, *arrays)

    def whole(*arrays):
        if devices != 16:
            return branch(4, *arrays)
        slots = arrays[-1]
        counts = jnp.sum(jnp.where(slots >= 0, 1 << (3 * (lax.iota(jnp.int32, slots.shape[0]) // 4)), 0))
        return lax.cond((counts & 0o44444444) == 0, functools.partial(branch, 3), functools.partial(branch, 4), *arrays)

    return jax.shard_map(
        whole,
        mesh=mesh,
        in_specs=(
            P(None, None, "module", None),
            P("module", "group", None, None),
            P("module", None, None),
            P("module", None, None),
            P("module", None, None),
            P(),
            P(),
        ),
        out_specs=P(None, "group"),
        check_vma=False,
    )
```
